128 devices in a mesh: dp: 8 (over z, y_lo), row: 2 (over y_hi), col: 8 (over x, core).
Axes of the slice: x: 4, y: 4 (y_hi: 2, y_lo: 2; y = y_hi * 2 + y_lo), z: 4, core: 2. Of those that a mesh axis runs over, the one named last changes fastest.
Arguments:
- layer_input: bfloat16 [8, 2048, 1024], P('dp', 'row', 'col'), may hold values from -6 to 6
- segment_ids: int32 [8, 2048], P('dp'), may hold values from 0 to 7, never falling along the last dimension, each value on 1 to 1024 neighbouring positions
- cotangent: bfloat16 [8, 2048, 1024], P('dp', 'row', 'col'), may hold values from -6 to 6
- norm1_gain: float32 [1024], P('col'), may hold values from 0.25 to 1.75
- norm1_bias: float32 [1024], P('col'), may hold values from -2 to 2
- norm2_gain: float32 [1024], P('col'), may hold values from 0.25 to 1.75
- norm2_bias: float32 [1024], P('col'), may hold values from -2 to 2
- w_qkv: bfloat16 [1024, 3072], P('col', 'row'), may hold values from -0.1875 to 0.1875
- b_qkv: float32 [3072], P(('row', 'col')), may hold values from -3 to 3
- w_out: bfloat16 [1024, 1024], P('row', 'col'), may hold values from -1.5 to 1.5
- w_up: bfloat16 [1024, 4096], P('col', 'row'), may hold values from -0.1875 to 0.1875
- b_up: float32 [4096], P(('row', 'col')), may hold values from -3 to 3
- w_down: bfloat16 [4096, 1024], P('row', 'col'), may hold values from -0.1875 to 0.1875
- out_bias: float32 [1024], P('col'), may hold values from -3 to 3
Outputs:
- layer_output: bfloat16 [8, 2048, 1024], P('dp', 'row', 'col')
- grad_input: float32 [8, 2048, 1024], P('dp', 'row', 'col')
- grad_w_qkv: float32 [1024, 3072], P('col', 'row')
- grad_b_qkv: float32 [3072], P(('row', 'col'))
- grad_w_out: float32 [1024, 1024], P('row', 'col')
- grad_w_up: float32 [1024, 4096], P('col', 'row')
- grad_b_up: float32 [4096], P(('row', 'col'))
- grad_w_down: float32 [4096, 1024], P('row', 'col')
- output_bias_gradient: float32 [1024], P('col')
- grad_norm1_gain: float32 [1024], P('col')
- grad_norm1_bias: float32 [1024], P('col')
- grad_norm2_gain: float32 [1024], P('col')
- grad_norm2_bias: float32 [1024], P('col')
The draws below stay inside these ranges and needn't reach their ends.
Inputs may be any that keep to these rules, and one draw needn't show every extreme that they name: `segment_ids`: document numbers never fall along a sequence; every document has 1 to 1024 positions and one document of each sequence has exactly 1024.
All inputs are finite; a program needn't handle non-finite values.
Results may differ from the reference program's by a relative error of at most 0.02.
Values may be sent and summed in bfloat16 or wider, within the bound.
No kernel may reach another device: no remote copies, remote signals or barrier semaphores. Data moves between devices by JAX's collectives and lax.ppermute only.
A program may use at most 192 MiB of HBM per device.

```python
import math
import jax
import jax.numpy as jnp
import numpy as np
from jax import lax

D = 1024
H = 16
FF = 4096
LEN = 2048
SEGS = 8
HD = 64
ROT = 16
SEQS = 8


def level_of(rng, shape, cuts, least, largest):
    factor_of = 1.0
    for axis_at, parts in cuts:
        steps = jax.random.uniform(jax.random.fold_in(jax.random.fold_in(rng, 6), axis_at), (parts,), jnp.float32, least / len(cuts), largest / len(cuts))
        factor_of = factor_of * jnp.repeat(jnp.exp(steps), shape[axis_at] // parts).reshape((-1,) + (1,) * (len(shape) - 1 - axis_at))
    return factor_of


def profile(number_of, total, most, slope):
    weights = [(1 << 20) // math.isqrt(grade ** slope) + 1 for grade in range(2, number_of + 1)]
    spare, given = total - most - (number_of - 1), [1] * (number_of - 1)
    while spare > 0:
        movable = [i for i in range(number_of - 1) if given[i] < most]
        pool, remaining = sum([weights[i] for i in movable]), spare
        for i in movable:
            more = min(most - given[i], max(1, remaining * weights[i] // pool), spare)
            given[i] = given[i] + more
            spare = spare - more
    return np.array([most] + given)


def uneven(key, amount, total, limit, slope):
    if amount == 2:
        one = jax.random.randint(key, (), max(1, total - limit), min(limit, total - 1) + 1)
        return jnp.stack([one, total - one])
    tallies = jnp.asarray(profile(amount, total, limit, slope), jnp.int32)
    twos = (amount - 1) // 2
    source_of, sink = tallies[1:1 + 2 * twos:2], tallies[2:2 + 2 * twos:2]
    slack = jnp.minimum(source_of - 1, limit - sink)
    passed = jax.random.randint(jax.random.fold_in(key, 1), (twos,), 0, 1 << 20) % (slack + 1)
    tallies = tallies.at[1:1 + 2 * twos:2].set(source_of - passed).at[2:2 + 2 * twos:2].set(sink + passed)
    return tallies[jax.random.permutation(jax.random.fold_in(key, 2), amount)]


def noise(stream_key, shape, deviation, bound, cuts=(), kind=jnp.bfloat16):
    loudness = level_of(stream_key, shape, cuts, -0.22, 0.18) if cuts else 1.0
    drawn = jax.random.normal(stream_key, shape, jnp.float32) * deviation * loudness
    return jnp.minimum(jnp.maximum(drawn, -bound), bound).astype(kind)


def setup_inputs(seed: int = 0) -> dict:
    key_of = jax.random.split(jax.random.key(seed), 15)
    layer_input = noise(key_of[0], (SEQS, LEN, D), 1.0, 6.0, ((0, 8), (1, 2), (2, 8)))
    segment_ids = jax.vmap(lambda own: jnp.searchsorted(jnp.cumsum(uneven(own, SEGS, LEN, LEN // 2, 1)), jnp.arange(LEN), side="right"))(jax.random.split(key_of[1], SEQS)).reshape((SEQS, LEN)).astype(jnp.int32)
    cotangent = noise(key_of[2], (SEQS, LEN, D), 1.0, 6.0, ((0, 8), (1, 2), (2, 8)))
    norm1_gain = jnp.clip(1.0 + 0.15 * jax.random.normal(key_of[3], (D,), jnp.float32), 0.25, 1.75)
    norm1_bias = noise(key_of[4], (D,), 0.4, 2.0, ((0, 8),), jnp.float32)
    norm2_gain = jnp.clip(1.0 + 0.15 * jax.random.normal(key_of[5], (D,), jnp.float32), 0.25, 1.75)
    norm2_bias = noise(key_of[6], (D,), 0.4, 2.0, ((0, 8),), jnp.float32)
    w_qkv = noise(key_of[7], (D, 3 * D), D ** -0.5, 0.1875, ((0, 8), (1, 2)))
    b_qkv = noise(key_of[8], (3 * D,), 0.5, 3.0, ((0, 16),), jnp.float32)
    w_out = noise(key_of[9], (D, D), (D // 64) ** -0.5, 1.5, ((0, 2), (1, 8)))
    w_up = noise(key_of[10], (D, FF), D ** -0.5, 0.1875, ((0, 8), (1, 2)))
    b_up = noise(key_of[11], (FF,), 0.5, 3.0, ((0, 16),), jnp.float32)
    w_down = noise(key_of[12], (FF, D), (FF // 4) ** -0.5, 0.1875, ((0, 2), (1, 8)))
    out_bias = noise(key_of[13], (D,), 0.5, 3.0, ((0, 8),), jnp.float32)
    return {"layer_input": layer_input, "segment_ids": segment_ids, "cotangent": cotangent, "norm1_gain": norm1_gain, "norm1_bias": norm1_bias, "norm2_gain": norm2_gain, "norm2_bias": norm2_bias, "w_qkv": w_qkv, "b_qkv": b_qkv, "w_out": w_out, "w_up": w_up, "b_up": b_up, "w_down": w_down, "out_bias": out_bias}


NORM_EPS = 1e-05

def rope_tables(length, rot_dims):
    half_dims = rot_dims // 2
    position = jnp.arange(length).astype(jnp.float32)
    freqs = 10000.0 ** (-jnp.arange(half_dims).astype(jnp.float32) * 2.0 / rot_dims)
    angles = position[:, None] * freqs[None, :]
    return (jnp.cos(angles), jnp.sin(angles))

def rotate(values, cosine, sine, rot_dims):
    half_dims = rot_dims // 2
    lower_half = values[..., :half_dims]
    upper_half = values[..., half_dims:rot_dims]
    cos_b = cosine[None, :, None, :]
    sin_b = sine[None, :, None, :]
    return jnp.concatenate([lower_half * cos_b - upper_half * sin_b, upper_half * cos_b + lower_half * sin_b, values[..., rot_dims:]], axis=-1)

def inverse_rotation(grads, cosine, sine, rot_dims):
    half_dims = rot_dims // 2
    lower_half = grads[..., :half_dims]
    upper_half = grads[..., half_dims:rot_dims]
    cos_b = cosine[None, :, None, :]
    sin_b = sine[None, :, None, :]
    return jnp.concatenate([lower_half * cos_b + upper_half * sin_b, upper_half * cos_b - lower_half * sin_b, grads[..., rot_dims:]], axis=-1)

def gelu_slope(values):
    cdf_part = 0.5 * (1.0 + lax.erf(values * (1.0 / math.sqrt(2.0))))
    return cdf_part + values * jnp.exp(-0.5 * values * values) * (1.0 / math.sqrt(2.0 * math.pi))

def block_mask(segment, offset, block_rows):
    length = segment.shape[1]
    position = jnp.arange(length)
    causal = position[offset:offset + block_rows, None] >= position[None, :]
    same_doc = segment[:, offset:offset + block_rows, None] == segment[:, None, :]
    return causal[None] & same_doc

def attend_forward(query, keys, values, segment, block_rows):
    length = query.shape[1]
    score_scale = query.shape[3] ** (-0.5)
    outputs = []
    totals = []
    for offset in range(0, length, block_rows):
        q_block = query[:, offset:offset + block_rows].astype(jnp.float32)
        scores = jnp.einsum('sqhd,skhd->shqk', q_block, keys.astype(jnp.float32)) * score_scale
        allowed = block_mask(segment, offset, block_rows)
        scores = jnp.where(allowed[:, None], scores, -jnp.inf)
        row_peak = lax.optimization_barrier(jnp.max(scores, axis=-1, keepdims=True))
        logsum = row_peak + jnp.log(lax.optimization_barrier(jnp.sum(jnp.exp(scores - row_peak), axis=-1, keepdims=True)))
        weights = jnp.exp(scores - logsum).astype(jnp.bfloat16)
        block_out = jnp.einsum('shqk,skhd->sqhd', weights.astype(jnp.float32), values.astype(jnp.float32))
        outputs.append(block_out.astype(jnp.bfloat16))
        totals.append(logsum[..., 0])
    return (jnp.concatenate(outputs, axis=1), jnp.concatenate(totals, axis=2))

def attend_backward(query, keys, values, attended, grad_att, logsum, segment, block_rows):
    length = query.shape[1]
    score_scale = query.shape[3] ** (-0.5)
    delta = lax.optimization_barrier(jnp.sum(grad_att.astype(jnp.float32) * attended.astype(jnp.float32), axis=-1))
    keys_f = keys.astype(jnp.float32)
    values_f = values.astype(jnp.float32)
    grad_keys = jnp.zeros(keys.shape, jnp.float32)
    grad_values = jnp.zeros(values.shape, jnp.float32)
    grad_query = []
    for offset in range(0, length, block_rows):
        q_block = query[:, offset:offset + block_rows].astype(jnp.float32)
        go_block = grad_att[:, offset:offset + block_rows].astype(jnp.float32)
        scores = jnp.einsum('sqhd,skhd->shqk', q_block, keys_f) * score_scale
        allowed = block_mask(segment, offset, block_rows)
        scores = jnp.where(allowed[:, None], scores, -jnp.inf)
        lse_block = logsum[:, :, offset:offset + block_rows]
        pexact = jnp.exp(scores - lse_block[..., None])
        probs = pexact.astype(jnp.bfloat16).astype(jnp.float32)
        grad_values = grad_values + jnp.einsum('shqk,sqhd->skhd', probs, go_block)
        grad_probs = jnp.einsum('sqhd,skhd->shqk', go_block, values_f)
        delta_block = jnp.transpose(delta[:, offset:offset + block_rows], (0, 2, 1))[..., None]
        grad_scores = (pexact * (grad_probs - delta_block)).astype(jnp.bfloat16).astype(jnp.float32)
        grad_query.append(jnp.einsum('shqk,skhd->sqhd', grad_scores, keys_f) * score_scale)
        grad_keys = grad_keys + jnp.einsum('shqk,sqhd->skhd', grad_scores, q_block) * score_scale
    return (jnp.concatenate(grad_query, axis=1), grad_keys, grad_values)

def reference(layer_input, segment_ids, cotangent, norm1_gain, norm1_bias, norm2_gain, norm2_bias, w_qkv, b_qkv, w_out, w_up, b_up, w_down, out_bias):
    block_rows = min(512, LEN)
    cosine, sine = rope_tables(LEN, ROT)

    def one_sequence(carry, items):
        seq_input, seq_segment, seq_grad = items
        x_float = seq_input.astype(jnp.float32)
        mean_val = lax.optimization_barrier(jnp.mean(x_float, axis=-1, keepdims=True))
        variance = lax.optimization_barrier(jnp.mean(x_float * x_float, axis=-1, keepdims=True)) - mean_val * mean_val
        inv_std = lax.rsqrt(variance + NORM_EPS)
        normed = (x_float - mean_val) * inv_std
        first_in = (normed * norm1_gain + norm1_bias).astype(jnp.bfloat16)
        second_in = (normed * norm2_gain + norm2_bias).astype(jnp.bfloat16)
        qkv = (jnp.dot(first_in, w_qkv, preferred_element_type=jnp.float32) + b_qkv).reshape(1, LEN, H, 3, HD)
        query = rotate(qkv[:, :, :, 0], cosine, sine, ROT).astype(jnp.bfloat16)
        keys = rotate(qkv[:, :, :, 1], cosine, sine, ROT).astype(jnp.bfloat16)
        values = qkv[:, :, :, 2].astype(jnp.bfloat16)
        segment = seq_segment[None]
        attended, logsum = attend_forward(query, keys, values, segment, block_rows)
        att_flat = attended.reshape(LEN, D)
        up_val = jnp.dot(second_in, w_up, preferred_element_type=jnp.float32) + b_up
        hidden = jax.nn.gelu(up_val, approximate=False).astype(jnp.bfloat16)
        branch = jnp.dot(att_flat, w_out, preferred_element_type=jnp.float32) + jnp.dot(hidden, w_down, preferred_element_type=jnp.float32) + out_bias
        layer_out = (x_float + branch).astype(jnp.bfloat16)
        grad_float = seq_grad.astype(jnp.float32)
        output_bias_grad_term = lax.optimization_barrier(jnp.sum(grad_float, axis=0))
        g_w_out = jnp.dot(att_flat.T, seq_grad, preferred_element_type=jnp.float32)
        g_w_down = jnp.dot(hidden.T, seq_grad, preferred_element_type=jnp.float32)
        grad_att = jnp.dot(seq_grad, w_out.T, preferred_element_type=jnp.float32).astype(jnp.bfloat16).reshape(1, LEN, H, HD)
        grad_up = jnp.dot(seq_grad, w_down.T, preferred_element_type=jnp.float32) * gelu_slope(up_val)
        grad_q, grad_k, grad_v = attend_backward(query, keys, values, attended, grad_att, logsum, segment, block_rows)
        grad_q = inverse_rotation(grad_q, cosine, sine, ROT)
        grad_k = inverse_rotation(grad_k, cosine, sine, ROT)
        grad_qkv = jnp.stack([grad_q, grad_k, grad_v], axis=3).reshape(LEN, 3 * D)
        g_b_qkv = lax.optimization_barrier(jnp.sum(grad_qkv, axis=0))
        g_b_up = lax.optimization_barrier(jnp.sum(grad_up, axis=0))
        qkv_round = grad_qkv.astype(jnp.bfloat16)
        up_round = grad_up.astype(jnp.bfloat16)
        g_w_qkv = jnp.dot(first_in.T, qkv_round, preferred_element_type=jnp.float32)
        g_w_up = jnp.dot(second_in.T, up_round, preferred_element_type=jnp.float32)
        grad_first = jnp.dot(qkv_round, w_qkv.T, preferred_element_type=jnp.float32)
        grad_second = jnp.dot(up_round, w_up.T, preferred_element_type=jnp.float32)
        g_n1g = lax.optimization_barrier(jnp.sum(grad_first * normed, axis=0))
        g_n1b = lax.optimization_barrier(jnp.sum(grad_first, axis=0))
        g_n2g = lax.optimization_barrier(jnp.sum(grad_second * normed, axis=0))
        g_n2b = lax.optimization_barrier(jnp.sum(grad_second, axis=0))
        grad_normed = grad_first * norm1_gain + grad_second * norm2_gain
        grad_in = grad_float + inv_std * (grad_normed - lax.optimization_barrier(jnp.mean(grad_normed, axis=-1, keepdims=True)) - normed * lax.optimization_barrier(jnp.mean(grad_normed * normed, axis=-1, keepdims=True)))
        terms = (g_w_qkv, g_b_qkv, g_w_out, g_w_up, g_b_up, g_w_down, output_bias_grad_term, g_n1g, g_n1b, g_n2g, g_n2b)
        carry = tuple((total + term for total, term in zip(carry, terms)))
        return (carry, (layer_out, grad_in))
    start_carry = (jnp.zeros((D, 3 * D), jnp.float32), jnp.zeros((3 * D,), jnp.float32), jnp.zeros((D, D), jnp.float32), jnp.zeros((D, FF), jnp.float32), jnp.zeros((FF,), jnp.float32), jnp.zeros((FF, D), jnp.float32), jnp.zeros((D,), jnp.float32), jnp.zeros((D,), jnp.float32), jnp.zeros((D,), jnp.float32), jnp.zeros((D,), jnp.float32), jnp.zeros((D,), jnp.float32))
    grads, (layer_output, grad_input) = lax.scan(one_sequence, start_carry, (layer_input, segment_ids, cotangent))
    return (layer_output, grad_input, grads[0], grads[1], grads[2], grads[3], grads[4], grads[5], grads[6], grads[7], grads[8], grads[9], grads[10])
```

```python
import math

import jax
import jax.numpy as jnp
from jax import lax
from jax.sharding import PartitionSpec as P

H = 16


NORM_EPS = 1e-05


def rope_tables(length, rot_dims):
    half_dims = rot_dims // 2
    position = jnp.arange(length).astype(jnp.float32)
    freqs = 10000.0 ** (-jnp.arange(half_dims).astype(jnp.float32) * 2.0 / rot_dims)
    angles = position[:, None] * freqs[None, :]
    return (jnp.cos(angles), jnp.sin(angles))


def rotate(values, cosine, sine, rot_dims):
    half_dims = rot_dims // 2
    lower_half = values[..., :half_dims]
    upper_half = values[..., half_dims:rot_dims]
    cos_b = cosine[None, :, None, :]
    sin_b = sine[None, :, None, :]
    return jnp.concatenate(
        [
            lower_half * cos_b - upper_half * sin_b,
            upper_half * cos_b + lower_half * sin_b,
            values[..., rot_dims:],
        ],
        axis=-1,
    )


def inverse_rotation(grads, cosine, sine, rot_dims):
    half_dims = rot_dims // 2
    lower_half = grads[..., :half_dims]
    upper_half = grads[..., half_dims:rot_dims]
    cos_b = cosine[None, :, None, :]
    sin_b = sine[None, :, None, :]
    return jnp.concatenate(
        [
            lower_half * cos_b + upper_half * sin_b,
            upper_half * cos_b - lower_half * sin_b,
            grads[..., rot_dims:],
        ],
        axis=-1,
    )


def gelu_slope(values):
    cdf_part = 0.5 * (1.0 + lax.erf(values * (1.0 / math.sqrt(2.0))))
    return cdf_part + values * jnp.exp(-0.5 * values * values) * (1.0 / math.sqrt(2.0 * math.pi))


def block_mask(segment, offset, block_rows):
    length = segment.shape[1]
    position = jnp.arange(length)
    causal = position[offset : offset + block_rows, None] >= position[None, :]
    same_doc = segment[:, offset : offset + block_rows, None] == segment[:, None, :]
    return causal[None] & same_doc


def attend_forward(query, keys, values, segment, block_rows):
    length = query.shape[1]
    score_scale = query.shape[3] ** (-0.5)
    outputs = []
    totals = []
    for offset in range(0, length, block_rows):
        q_block = query[:, offset : offset + block_rows]
        scores = (
            jnp.einsum("sqhd,skhd->shqk", q_block, keys, preferred_element_type=jnp.float32)
            * score_scale
        )
        allowed = block_mask(segment, offset, block_rows)
        scores = jnp.where(allowed[:, None], scores, -jnp.inf)
        row_peak = jnp.max(scores, axis=-1, keepdims=True)
        logsum = row_peak + jnp.log(jnp.sum(jnp.exp(scores - row_peak), axis=-1, keepdims=True))
        weights = jnp.exp(scores - logsum).astype(jnp.bfloat16)
        block_out = jnp.einsum(
            "shqk,skhd->sqhd", weights, values, preferred_element_type=jnp.float32
        )
        outputs.append(block_out.astype(jnp.bfloat16))
        totals.append(logsum[..., 0])
    return (jnp.concatenate(outputs, axis=1), jnp.concatenate(totals, axis=2))


def attend_backward(query, keys, values, attended, grad_att, logsum, segment, block_rows):
    length = query.shape[1]
    score_scale = query.shape[3] ** (-0.5)
    delta = jnp.sum(grad_att.astype(jnp.float32) * attended.astype(jnp.float32), axis=-1)
    grad_keys = jnp.zeros(keys.shape, jnp.float32)
    grad_values = jnp.zeros(values.shape, jnp.float32)
    grad_query = []
    for offset in range(0, length, block_rows):
        q_block = query[:, offset : offset + block_rows]
        go_block = grad_att[:, offset : offset + block_rows]
        scores = (
            jnp.einsum("sqhd,skhd->shqk", q_block, keys, preferred_element_type=jnp.float32)
            * score_scale
        )
        allowed = block_mask(segment, offset, block_rows)
        scores = jnp.where(allowed[:, None], scores, -jnp.inf)
        lse_block = logsum[:, :, offset : offset + block_rows]
        pexact = jnp.exp(scores - lse_block[..., None])
        probs = pexact.astype(jnp.bfloat16)
        grad_values = grad_values + jnp.einsum(
            "shqk,sqhd->skhd", probs, go_block, preferred_element_type=jnp.float32
        )
        grad_probs = jnp.einsum(
            "sqhd,skhd->shqk", go_block, values, preferred_element_type=jnp.float32
        )
        delta_block = jnp.transpose(delta[:, offset : offset + block_rows], (0, 2, 1))[..., None]
        grad_scores = (pexact * (grad_probs - delta_block)).astype(jnp.bfloat16)
        grad_query.append(
            jnp.einsum("shqk,skhd->sqhd", grad_scores, keys, preferred_element_type=jnp.float32)
            * score_scale
        )
        grad_keys = (
            grad_keys
            + jnp.einsum(
                "shqk,sqhd->skhd", grad_scores, q_block, preferred_element_type=jnp.float32
            )
            * score_scale
        )
    return (jnp.concatenate(grad_query, axis=1), grad_keys, grad_values)


def gather_grid(block):
    row_count = lax.axis_size("row")
    col_count = lax.axis_size("col")
    _, rows_here, feats_here = block.shape
    stacked = lax.all_gather(block[0], ("row", "col"), axis=0, tiled=False)
    stacked = stacked.reshape(row_count, col_count, rows_here, feats_here)
    return stacked.transpose(0, 2, 1, 3).reshape(row_count * rows_here, col_count * feats_here)


def scatter_grid(full, rows_here, feats_here):
    row_count = lax.axis_size("row")
    col_count = lax.axis_size("col")
    blocks = full.reshape(row_count, rows_here, col_count, feats_here).transpose(0, 2, 1, 3)
    blocks = blocks.reshape(row_count * col_count, rows_here, feats_here)
    return lax.psum_scatter(blocks, ("row", "col"), scatter_dimension=0, tiled=True)[0]


def local(
    layer_input,
    segment_ids,
    cotangent,
    norm1_gain,
    norm1_bias,
    norm2_gain,
    norm2_bias,
    w_qkv,
    b_qkv,
    w_out,
    w_up,
    b_up,
    w_down,
    out_bias,
):
    col_count = lax.axis_size("col")
    row_index = lax.axis_index("row")
    col_index = lax.axis_index("col")
    seq_count, rows_here, feat_here = layer_input.shape
    full_len = segment_ids.shape[1]
    model_width = feat_here * col_count
    head_dim = model_width // H
    rot_dims = head_dim // 4
    heads_here = b_qkv.shape[0] // (3 * head_dim)
    att_width = heads_here * head_dim
    qkv_here = b_qkv.shape[0]
    units_here = b_up.shape[0]
    block_rows = min(512, full_len)

    w_in_parts = jnp.concatenate(
        [
            w_qkv.reshape(feat_here, col_count, qkv_here),
            w_up.reshape(feat_here, col_count, units_here),
        ],
        axis=2,
    )
    w_in_cols = lax.all_to_all(w_in_parts, "col", 1, 0, tiled=True).reshape(model_width, -1)
    w_qkv_cols = w_in_cols[:, :qkv_here]
    w_up_cols = w_in_cols[:, qkv_here:]
    w_back_parts = jnp.concatenate(
        [
            w_out.reshape(col_count, att_width, feat_here),
            w_down.reshape(col_count, units_here, feat_here),
        ],
        axis=1,
    )
    stacked_w = lax.all_to_all(w_back_parts, "col", 0, 2, tiled=True).reshape(-1, model_width)
    norm_params = lax.all_gather(
        jnp.stack([norm1_gain, norm1_bias, norm2_gain, norm2_bias]), "col", axis=1, tiled=True
    )
    gain1, bias1, gain2, bias2 = norm_params[0], norm_params[1], norm_params[2], norm_params[3]

    x_full = gather_grid(layer_input).astype(jnp.float32)
    mean_val = jnp.mean(x_full, axis=1, keepdims=True)
    variance = jnp.mean(x_full * x_full, axis=1, keepdims=True) - mean_val * mean_val
    inv_std = lax.rsqrt(variance + NORM_EPS)
    normed = (x_full - mean_val) * inv_std
    first_in = (normed * gain1 + bias1).astype(jnp.bfloat16)
    second_in = (normed * gain2 + bias2).astype(jnp.bfloat16)
    qkv_sum = jnp.dot(first_in, w_qkv_cols, preferred_element_type=jnp.float32)
    up_sum = jnp.dot(second_in, w_up_cols, preferred_element_type=jnp.float32)
    cosine, sine = rope_tables(full_len, rot_dims)
    qkv = (qkv_sum + b_qkv).reshape(seq_count, full_len, heads_here, 3, head_dim)
    query = rotate(qkv[:, :, :, 0], cosine, sine, rot_dims).astype(jnp.bfloat16)
    keys = rotate(qkv[:, :, :, 1], cosine, sine, rot_dims).astype(jnp.bfloat16)
    values = qkv[:, :, :, 2].astype(jnp.bfloat16)
    attended, logsum = attend_forward(query, keys, values, segment_ids, block_rows)
    up_val = up_sum + b_up
    hidden = jax.nn.gelu(up_val, approximate=False).astype(jnp.bfloat16)
    joined = jnp.concatenate([attended.reshape(full_len, att_width), hidden], axis=1)
    branch_part = jnp.dot(joined, stacked_w, preferred_element_type=jnp.float32)
    branch_sum = scatter_grid(branch_part.astype(jnp.bfloat16), rows_here, feat_here)
    layer_output = (
        layer_input[0].astype(jnp.float32) + branch_sum.astype(jnp.float32) + out_bias
    ).astype(jnp.bfloat16)[None]

    cot_full = gather_grid(cotangent)
    grad_stacked = jnp.dot(joined.T, cot_full, preferred_element_type=jnp.float32)
    joined_grad = jnp.dot(cot_full, stacked_w.T, preferred_element_type=jnp.float32)
    grad_att = joined_grad[:, :att_width].astype(jnp.bfloat16).reshape(
        seq_count, full_len, heads_here, head_dim
    )
    grad_up = joined_grad[:, att_width:] * gelu_slope(up_val)
    grad_q, grad_k, grad_v = attend_backward(
        query, keys, values, attended, grad_att, logsum, segment_ids, block_rows
    )
    grad_q = inverse_rotation(grad_q, cosine, sine, rot_dims)
    grad_k = inverse_rotation(grad_k, cosine, sine, rot_dims)
    grad_qkv = jnp.stack([grad_q, grad_k, grad_v], axis=3).reshape(full_len, qkv_here)
    grad_b_qkv = jnp.sum(grad_qkv, axis=0)
    grad_b_up = jnp.sum(grad_up, axis=0)
    qkv_round = grad_qkv.astype(jnp.bfloat16)
    up_round = grad_up.astype(jnp.bfloat16)
    grad_w_qkv = jnp.dot(first_in.T, qkv_round, preferred_element_type=jnp.float32)
    grad_w_up = jnp.dot(second_in.T, up_round, preferred_element_type=jnp.float32)
    part_first = jnp.dot(qkv_round, w_qkv_cols.T, preferred_element_type=jnp.float32)
    part_second = jnp.dot(up_round, w_up_cols.T, preferred_element_type=jnp.float32)
    part_normed = part_first * gain1 + part_second * gain2
    normed_sums = lax.psum(
        jnp.stack([jnp.sum(part_normed, axis=1), jnp.sum(part_normed * normed, axis=1)]),
        ("row", "col"),
    )
    grad_normed = scatter_grid(part_normed.astype(jnp.bfloat16), rows_here, feat_here)

    cot_sum = jnp.sum(cotangent[0].astype(jnp.float32), axis=0)
    placed_cot_sum = jnp.zeros((col_count, feat_here), jnp.float32)
    placed_cot_sum = lax.dynamic_update_slice(placed_cot_sum, cot_sum[None], (col_index, 0))
    vector_sums = lax.psum(
        jnp.stack(
            [
                jnp.sum(part_first * normed, axis=0),
                jnp.sum(part_first, axis=0),
                jnp.sum(part_second * normed, axis=0),
                jnp.sum(part_second, axis=0),
                placed_cot_sum.reshape(model_width),
            ]
        ),
        ("dp", "row", "col"),
    )
    vector_here = lax.dynamic_slice(vector_sums, (0, col_index * feat_here), (5, feat_here))

    row_start = row_index * rows_here
    normed_here = lax.dynamic_slice(
        normed, (row_start, col_index * feat_here), (rows_here, feat_here)
    )
    inv_std_here = lax.dynamic_slice(inv_std, (row_start, 0), (rows_here, 1))
    sums_here = lax.dynamic_slice(normed_sums, (0, row_start), (2, rows_here))
    grad_input = cotangent[0].astype(jnp.float32) + inv_std_here * (
        grad_normed.astype(jnp.float32)
        - (sums_here[0] / model_width)[:, None]
        - normed_here * (sums_here[1] / model_width)[:, None]
    )

    in_grads = jnp.concatenate([grad_w_qkv, grad_w_up], axis=1).astype(jnp.bfloat16)
    back_grads = grad_stacked.astype(jnp.bfloat16)
    in_grads, back_grads, bias_qkv_sum, bias_up_sum = lax.psum(
        (in_grads, back_grads, grad_b_qkv.astype(jnp.bfloat16), grad_b_up.astype(jnp.bfloat16)),
        "dp",
    )
    in_grads = lax.all_to_all(
        in_grads.reshape(model_width, 1, -1), "col", 0, 1, tiled=True
    ).astype(jnp.float32)
    back_grads = lax.all_to_all(
        back_grads.reshape(1, -1, model_width), "col", 2, 0, tiled=True
    ).astype(jnp.float32)
    grad_w_qkv_out = in_grads[:, :, :qkv_here].reshape(feat_here, -1)
    grad_w_up_out = in_grads[:, :, qkv_here:].reshape(feat_here, -1)
    grad_w_out_out = back_grads[:, :att_width].reshape(-1, feat_here)
    grad_w_down_out = back_grads[:, att_width:].reshape(-1, feat_here)
    return (
        layer_output,
        grad_input[None],
        grad_w_qkv_out,
        bias_qkv_sum.astype(jnp.float32),
        grad_w_out_out,
        grad_w_up_out,
        bias_up_sum.astype(jnp.float32),
        grad_w_down_out,
        vector_here[4],
        vector_here[0],
        vector_here[1],
        vector_here[2],
        vector_here[3],
    )


def solution(mesh):
    in_specs = (
        P("dp", "row", "col"),
        P("dp", None),
        P("dp", "row", "col"),
        P("col"),
        P("col"),
        P("col"),
        P("col"),
        P("col", "row"),
        P(("row", "col")),
        P("row", "col"),
        P("col", "row"),
        P(("row", "col")),
        P("row", "col"),
        P("col"),
    )
    out_specs = (
        P("dp", "row", "col"),
        P("dp", "row", "col"),
        P("col", "row"),
        P(("row", "col")),
        P("row", "col"),
        P("col", "row"),
        P(("row", "col")),
        P("row", "col"),
        P("col"),
        P("col"),
        P("col"),
        P("col"),
        P("col"),
    )
    return jax.shard_map(local, mesh=mesh, in_specs=in_specs, out_specs=out_specs, check_vma=False)
```

```python
import math

import jax
import jax.numpy as jnp
from jax import lax
from jax.sharding import PartitionSpec as P

H = 16


NORM_EPS = 1e-05


def rope_tables(length, rot_dims):
    half_dims = rot_dims // 2
    position = jnp.arange(length).astype(jnp.float32)
    freqs = 10000.0 ** (-jnp.arange(half_dims).astype(jnp.float32) * 2.0 / rot_dims)
    angles = position[:, None] * freqs[None, :]
    return (jnp.cos(angles), jnp.sin(angles))


def rotate(values, cosine, sine, rot_dims):
    half_dims = rot_dims // 2
    lower_half = values[..., :half_dims]
    upper_half = values[..., half_dims:rot_dims]
    cos_b = cosine[None, :, None, :]
    sin_b = sine[None, :, None, :]
    return jnp.concatenate(
        [
            lower_half * cos_b - upper_half * sin_b,
            upper_half * cos_b + lower_half * sin_b,
            values[..., rot_dims:],
        ],
        axis=-1,
    )


def inverse_rotation(grads, cosine, sine, rot_dims):
    half_dims = rot_dims // 2
    lower_half = grads[..., :half_dims]
    upper_half = grads[..., half_dims:rot_dims]
    cos_b = cosine[None, :, None, :]
    sin_b = sine[None, :, None, :]
    return jnp.concatenate(
        [
            lower_half * cos_b + upper_half * sin_b,
            upper_half * cos_b - lower_half * sin_b,
            grads[..., rot_dims:],
        ],
        axis=-1,
    )


def gelu_slope(values):
    cdf_part = 0.5 * (1.0 + lax.erf(values * (1.0 / math.sqrt(2.0))))
    return cdf_part + values * jnp.exp(-0.5 * values * values) * (1.0 / math.sqrt(2.0 * math.pi))


def block_mask(segment, offset, block_rows):
    length = segment.shape[1]
    position = jnp.arange(length)
    causal = position[offset : offset + block_rows, None] >= position[None, :]
    same_doc = segment[:, offset : offset + block_rows, None] == segment[:, None, :]
    return causal[None] & same_doc


def attend_forward(query, keys, values, segment, block_rows):
    length = query.shape[1]
    score_scale = query.shape[3] ** (-0.5)
    outputs = []
    totals = []
    for offset in range(0, length, block_rows):
        q_block = query[:, offset : offset + block_rows]
        scores = (
            jnp.einsum("sqhd,skhd->shqk", q_block, keys, preferred_element_type=jnp.float32)
            * score_scale
        )
        allowed = block_mask(segment, offset, block_rows)
        scores = jnp.where(allowed[:, None], scores, -jnp.inf)
        row_peak = jnp.max(scores, axis=-1, keepdims=True)
        logsum = row_peak + jnp.log(jnp.sum(jnp.exp(scores - row_peak), axis=-1, keepdims=True))
        weights = jnp.exp(scores - logsum).astype(jnp.bfloat16)
        block_out = jnp.einsum(
            "shqk,skhd->sqhd", weights, values, preferred_element_type=jnp.float32
        )
        outputs.append(block_out.astype(jnp.bfloat16))
        totals.append(logsum[..., 0])
    return (jnp.concatenate(outputs, axis=1), jnp.concatenate(totals, axis=2))


def attend_backward(query, keys, values, attended, grad_att, logsum, segment, block_rows):
    length = query.shape[1]
    score_scale = query.shape[3] ** (-0.5)
    delta = jnp.sum(grad_att.astype(jnp.float32) * attended.astype(jnp.float32), axis=-1)
    grad_keys = jnp.zeros(keys.shape, jnp.float32)
    grad_values = jnp.zeros(values.shape, jnp.float32)
    grad_query = []
    for offset in range(0, length, block_rows):
        q_block = query[:, offset : offset + block_rows]
        go_block = grad_att[:, offset : offset + block_rows]
        scores = (
            jnp.einsum("sqhd,skhd->shqk", q_block, keys, preferred_element_type=jnp.float32)
            * score_scale
        )
        allowed = block_mask(segment, offset, block_rows)
        scores = jnp.where(allowed[:, None], scores, -jnp.inf)
        lse_block = logsum[:, :, offset : offset + block_rows]
        pexact = jnp.exp(scores - lse_block[..., None])
        probs = pexact.astype(jnp.bfloat16)
        grad_values = grad_values + jnp.einsum(
            "shqk,sqhd->skhd", probs, go_block, preferred_element_type=jnp.float32
        )
        grad_probs = jnp.einsum(
            "sqhd,skhd->shqk", go_block, values, preferred_element_type=jnp.float32
        )
        delta_block = jnp.transpose(delta[:, offset : offset + block_rows], (0, 2, 1))[..., None]
        grad_scores = (pexact * (grad_probs - delta_block)).astype(jnp.bfloat16)
        grad_query.append(
            jnp.einsum("shqk,skhd->sqhd", grad_scores, keys, preferred_element_type=jnp.float32)
            * score_scale
        )
        grad_keys = (
            grad_keys
            + jnp.einsum(
                "shqk,sqhd->skhd", grad_scores, q_block, preferred_element_type=jnp.float32
            )
            * score_scale
        )
    return (jnp.concatenate(grad_query, axis=1), grad_keys, grad_values)


def split_three(values):
    high = lax.reduce_precision(values, exponent_bits=8, mantissa_bits=7)
    rest = values - high
    middle = lax.reduce_precision(rest, exponent_bits=8, mantissa_bits=7)
    low = rest - middle
    return jnp.stack([high, middle, low]).astype(jnp.bfloat16)


def join_three(parts):
    parts = parts.astype(jnp.float32)
    return (parts[0] + parts[1]) + parts[2]


def sum_over_dp(tree):
    dp_count = lax.axis_size("dp")
    step = 1
    while step < dp_count:
        pairs = [(i, i ^ step) for i in range(dp_count)]
        other = lax.ppermute(tree, "dp", pairs)
        tree = jax.tree.map(
            lambda mine, theirs: (mine.astype(jnp.float32) + theirs.astype(jnp.float32)).astype(
                mine.dtype
            ),
            tree,
            other,
        )
        step *= 2
    return tree


def local(
    layer_input,
    segment_ids,
    cotangent,
    norm1_gain,
    norm1_bias,
    norm2_gain,
    norm2_bias,
    w_qkv,
    b_qkv,
    w_out,
    w_up,
    b_up,
    w_down,
    out_bias,
):
    col_count = lax.axis_size("col")
    row_count = lax.axis_size("row")
    row_index = lax.axis_index("row")
    col_index = lax.axis_index("col")
    seq_count, rows_here, feat_here = layer_input.shape
    full_len = segment_ids.shape[1]
    model_width = feat_here * col_count
    head_dim = model_width // H
    rot_dims = head_dim // 4
    heads_here = b_qkv.shape[0] // (3 * head_dim)
    att_width = heads_here * head_dim
    qkv_here = b_qkv.shape[0]
    units_here = b_up.shape[0]
    in_width = qkv_here + units_here
    block_rows = min(512, full_len)
    pad_rows = 16

    w_in_parts = jnp.concatenate(
        [
            w_qkv.reshape(feat_here, col_count, qkv_here),
            w_up.reshape(feat_here, col_count, units_here),
        ],
        axis=2,
    )
    w_in_cols = lax.all_to_all(w_in_parts, "col", 1, 0, tiled=True).reshape(model_width, -1)
    w_qkv_cols = w_in_cols[:, :qkv_here]
    w_up_cols = w_in_cols[:, qkv_here:]
    w_back_parts = jnp.concatenate(
        [
            w_out.reshape(col_count, att_width, feat_here),
            w_down.reshape(col_count, units_here, feat_here),
        ],
        axis=1,
    )
    stacked_w = lax.all_to_all(w_back_parts, "col", 0, 2, tiled=True).reshape(-1, model_width)

    norm_code = split_three(jnp.stack([norm1_gain, norm1_bias, norm2_gain, norm2_bias]))
    norm_code = norm_code.reshape(12, feat_here)
    block = jnp.concatenate(
        [
            layer_input[0],
            cotangent[0],
            norm_code,
            jnp.zeros((pad_rows - 12, feat_here), jnp.bfloat16),
        ],
        axis=0,
    )
    gathered = lax.all_gather(block, ("row", "col"), axis=0, tiled=False)
    gathered = gathered.reshape(row_count, col_count, -1, feat_here)
    x_b = gathered[:, :, :rows_here].astype(jnp.float32)
    cot_b = gathered[:, :, rows_here : 2 * rows_here]
    norm_all = gathered[0, :, 2 * rows_here : 2 * rows_here + 12].transpose(1, 0, 2)
    norm_vals = join_three(norm_all.reshape(3, 4, col_count, 1, feat_here))
    gain1, bias1, gain2, bias2 = norm_vals[0], norm_vals[1], norm_vals[2], norm_vals[3]

    mean_val = jnp.mean(x_b, axis=(1, 3), keepdims=True)
    variance = jnp.mean(x_b * x_b, axis=(1, 3), keepdims=True) - mean_val * mean_val
    inv_std = lax.rsqrt(variance + NORM_EPS)
    normed = (x_b - mean_val) * inv_std
    first_in = (normed * gain1 + bias1).astype(jnp.bfloat16)
    second_in = (normed * gain2 + bias2).astype(jnp.bfloat16)
    w_qkv_b = w_qkv_cols.reshape(col_count, feat_here, qkv_here)
    w_up_b = w_up_cols.reshape(col_count, feat_here, units_here)
    stacked_b = stacked_w.reshape(-1, col_count, feat_here)
    qkv_sum = jnp.einsum("rcpf,cfk->rpk", first_in, w_qkv_b, preferred_element_type=jnp.float32)
    up_sum = jnp.einsum("rcpf,cfu->rpu", second_in, w_up_b, preferred_element_type=jnp.float32)
    cosine, sine = rope_tables(full_len, rot_dims)
    qkv = (qkv_sum + b_qkv).reshape(seq_count, full_len, heads_here, 3, head_dim)
    query = rotate(qkv[:, :, :, 0], cosine, sine, rot_dims).astype(jnp.bfloat16)
    keys = rotate(qkv[:, :, :, 1], cosine, sine, rot_dims).astype(jnp.bfloat16)
    values = qkv[:, :, :, 2].astype(jnp.bfloat16)
    attended, logsum = attend_forward(query, keys, values, segment_ids, block_rows)
    up_val = (up_sum + b_up).reshape(full_len, units_here)
    hidden = jax.nn.gelu(up_val, approximate=False).astype(jnp.bfloat16)
    joined = jnp.concatenate([attended.reshape(full_len, att_width), hidden], axis=1)
    joined = joined.reshape(row_count, rows_here, -1)
    branch_blocks = jnp.einsum(
        "rpm,mcf->rcpf", joined, stacked_b, preferred_element_type=jnp.float32
    ).astype(jnp.bfloat16)
    branch_sum = lax.psum_scatter(
        branch_blocks.reshape(row_count * col_count, rows_here, feat_here),
        ("row", "col"),
        scatter_dimension=0,
        tiled=True,
    )[0]
    layer_output = (
        layer_input[0].astype(jnp.float32) + branch_sum.astype(jnp.float32) + out_bias
    ).astype(jnp.bfloat16)[None]

    grad_stacked = jnp.einsum("rpm,rcpf->mcf", joined, cot_b, preferred_element_type=jnp.float32)
    joined_grad = jnp.einsum(
        "rcpf,mcf->rpm", cot_b, stacked_b, preferred_element_type=jnp.float32
    ).reshape(full_len, -1)
    grad_att = joined_grad[:, :att_width].astype(jnp.bfloat16).reshape(
        seq_count, full_len, heads_here, head_dim
    )
    grad_up = joined_grad[:, att_width:] * gelu_slope(up_val)
    grad_b_up = jnp.sum(grad_up, axis=0)
    up_round = grad_up.astype(jnp.bfloat16).reshape(row_count, rows_here, units_here)
    grad_w_up = jnp.einsum("rcpf,rpu->cfu", second_in, up_round, preferred_element_type=jnp.float32)

    up_grads = lax.all_to_all(
        grad_w_up.astype(jnp.bfloat16).reshape(model_width, 1, units_here), "col", 0, 1, tiled=True
    )
    back_grads = lax.all_to_all(
        grad_stacked.astype(jnp.bfloat16).reshape(1, -1, model_width), "col", 2, 0, tiled=True
    )
    up_grads, back_grads, grad_b_up = sum_over_dp((up_grads, back_grads, grad_b_up))

    grad_q, grad_k, grad_v = attend_backward(
        query, keys, values, attended, grad_att, logsum, segment_ids, block_rows
    )
    grad_q = inverse_rotation(grad_q, cosine, sine, rot_dims)
    grad_k = inverse_rotation(grad_k, cosine, sine, rot_dims)
    grad_qkv = jnp.stack([grad_q, grad_k, grad_v], axis=3).reshape(full_len, qkv_here)
    grad_b_qkv = jnp.sum(grad_qkv, axis=0)
    qkv_round = grad_qkv.astype(jnp.bfloat16).reshape(row_count, rows_here, qkv_here)
    grad_w_qkv = jnp.einsum(
        "rcpf,rpk->cfk", first_in, qkv_round, preferred_element_type=jnp.float32
    )
    part_first = jnp.einsum("rpk,cfk->rcpf", qkv_round, w_qkv_b, preferred_element_type=jnp.float32)
    part_second = jnp.einsum("rpu,cfu->rcpf", up_round, w_up_b, preferred_element_type=jnp.float32)
    part_normed = part_first * gain1 + part_second * gain2

    gain_parts = jnp.stack(
        [
            jnp.sum(part_first * normed, axis=(0, 2)),
            jnp.sum(part_first, axis=(0, 2)),
            jnp.sum(part_second * normed, axis=(0, 2)),
            jnp.sum(part_second, axis=(0, 2)),
        ]
    )
    stat_rows = 2 * rows_here // feat_here
    stat_parts = jnp.stack(
        [jnp.sum(part_normed, axis=(1, 3)), jnp.sum(part_normed * normed, axis=(1, 3))], axis=1
    ).reshape(row_count, 1, stat_rows, feat_here)
    extra_rows = -(-(4 + stat_rows) // pad_rows) * pad_rows
    extras = jnp.concatenate(
        [
            jnp.broadcast_to(
                gain_parts.transpose(1, 0, 2)[None], (row_count, col_count, 4, feat_here)
            ),
            jnp.broadcast_to(stat_parts, (row_count, col_count, stat_rows, feat_here)),
            jnp.zeros(
                (row_count, col_count, extra_rows - 4 - stat_rows, feat_here), jnp.float32
            ),
        ],
        axis=2,
    ).astype(jnp.bfloat16)
    normed_blocks = jnp.concatenate([part_normed.astype(jnp.bfloat16), extras], axis=2)
    normed_blocks = normed_blocks.reshape(row_count * col_count, -1, feat_here)
    normed_sum = lax.psum_scatter(normed_blocks, ("row", "col"), scatter_dimension=0, tiled=True)[0]
    grad_normed = normed_sum[:rows_here].astype(jnp.float32)
    gain_sums = normed_sum[rows_here : rows_here + 4].astype(jnp.float32)
    stat_sums = normed_sum[rows_here + 4 : rows_here + 4 + stat_rows].astype(jnp.float32)
    stat_sums = stat_sums.reshape(2, rows_here)

    col_index = lax.axis_index("col")
    normed_here = lax.dynamic_slice(
        normed, (row_index, col_index, 0, 0), (1, 1, rows_here, feat_here)
    )[0, 0]
    inv_std_here = lax.dynamic_slice_in_dim(inv_std, row_index, 1, axis=0)[0, 0]
    grad_input = cotangent[0].astype(jnp.float32) + inv_std_here * (
        grad_normed
        - (stat_sums[0] / model_width)[:, None]
        - normed_here * (stat_sums[1] / model_width)[:, None]
    )

    cot_sum = lax.dynamic_slice_in_dim(
        jnp.sum(cot_b.astype(jnp.float32), axis=(0, 2)), col_index, 1, axis=0
    )[0]
    qkv_grads = lax.all_to_all(
        grad_w_qkv.astype(jnp.bfloat16).reshape(model_width, 1, qkv_here), "col", 0, 1, tiled=True
    )
    small = jnp.concatenate([grad_b_qkv, gain_sums.reshape(-1), cot_sum])
    qkv_grads, small = sum_over_dp((qkv_grads, small))
    up_grads = up_grads.astype(jnp.float32)
    qkv_grads = qkv_grads.astype(jnp.float32)
    back_grads = back_grads.astype(jnp.float32)
    grad_w_qkv_out = qkv_grads.reshape(feat_here, -1)
    grad_w_up_out = up_grads.reshape(feat_here, -1)
    grad_w_out_out = back_grads[:, :att_width].reshape(-1, feat_here)
    grad_w_down_out = back_grads[:, att_width:].reshape(-1, feat_here)
    vector_sums = small[qkv_here:].reshape(5, feat_here)
    return (
        layer_output,
        grad_input[None],
        grad_w_qkv_out,
        small[:qkv_here],
        grad_w_out_out,
        grad_w_up_out,
        grad_b_up,
        grad_w_down_out,
        vector_sums[4],
        vector_sums[0],
        vector_sums[1],
        vector_sums[2],
        vector_sums[3],
    )


def solution(mesh):
    in_specs = (
        P("dp", "row", "col"),
        P("dp", None),
        P("dp", "row", "col"),
        P("col"),
        P("col"),
        P("col"),
        P("col"),
        P("col", "row"),
        P(("row", "col")),
        P("row", "col"),
        P("col", "row"),
        P(("row", "col")),
        P("row", "col"),
        P("col"),
    )
    out_specs = (
        P("dp", "row", "col"),
        P("dp", "row", "col"),
        P("col", "row"),
        P(("row", "col")),
        P("row", "col"),
        P("col", "row"),
        P(("row", "col")),
        P("row", "col"),
        P("col"),
        P("col"),
        P("col"),
        P("col"),
        P("col"),
    )
    return jax.shard_map(local, mesh=mesh, in_specs=in_specs, out_specs=out_specs, check_vma=False)
```

```python
import math

import jax
import jax.numpy as jnp
from jax import lax
from jax.sharding import PartitionSpec as P

H = 16


NORM_EPS = 1e-05


def rope_tables(length, rot_dims):
    half_dims = rot_dims // 2
    position = jnp.arange(length).astype(jnp.float32)
    freqs = 10000.0 ** (-jnp.arange(half_dims).astype(jnp.float32) * 2.0 / rot_dims)
    angles = position[:, None] * freqs[None, :]
    return (jnp.cos(angles), jnp.sin(angles))


def rotate(values, cosine, sine, rot_dims):
    half_dims = rot_dims // 2
    lower_half = values[..., :half_dims]
    upper_half = values[..., half_dims:rot_dims]
    cos_b = cosine[None, :, None, :]
    sin_b = sine[None, :, None, :]
    return jnp.concatenate(
        [
            lower_half * cos_b - upper_half * sin_b,
            upper_half * cos_b + lower_half * sin_b,
            values[..., rot_dims:],
        ],
        axis=-1,
    )


def inverse_rotation(grads, cosine, sine, rot_dims):
    half_dims = rot_dims // 2
    lower_half = grads[..., :half_dims]
    upper_half = grads[..., half_dims:rot_dims]
    cos_b = cosine[None, :, None, :]
    sin_b = sine[None, :, None, :]
    return jnp.concatenate(
        [
            lower_half * cos_b + upper_half * sin_b,
            upper_half * cos_b - lower_half * sin_b,
            grads[..., rot_dims:],
        ],
        axis=-1,
    )


def gelu_slope(values):
    cdf_part = 0.5 * (1.0 + lax.erf(values * (1.0 / math.sqrt(2.0))))
    return cdf_part + values * jnp.exp(-0.5 * values * values) * (1.0 / math.sqrt(2.0 * math.pi))


def block_mask(segment, offset, block_rows):
    length = segment.shape[1]
    position = jnp.arange(length)
    causal = position[offset : offset + block_rows, None] >= position[None, :]
    same_doc = segment[:, offset : offset + block_rows, None] == segment[:, None, :]
    return causal[None] & same_doc


def attend_forward(query, keys, values, segment, block_rows):
    length = query.shape[1]
    score_scale = query.shape[3] ** (-0.5)
    outputs = []
    totals = []
    for offset in range(0, length, block_rows):
        q_block = query[:, offset : offset + block_rows]
        scores = (
            jnp.einsum("sqhd,skhd->shqk", q_block, keys, preferred_element_type=jnp.float32)
            * score_scale
        )
        allowed = block_mask(segment, offset, block_rows)
        scores = jnp.where(allowed[:, None], scores, -jnp.inf)
        row_peak = jnp.max(scores, axis=-1, keepdims=True)
        logsum = row_peak + jnp.log(jnp.sum(jnp.exp(scores - row_peak), axis=-1, keepdims=True))
        weights = jnp.exp(scores - logsum).astype(jnp.bfloat16)
        block_out = jnp.einsum(
            "shqk,skhd->sqhd", weights, values, preferred_element_type=jnp.float32
        )
        outputs.append(block_out.astype(jnp.bfloat16))
        totals.append(logsum[..., 0])
    return (jnp.concatenate(outputs, axis=1), jnp.concatenate(totals, axis=2))


def attend_backward(query, keys, values, attended, grad_att, logsum, segment, block_rows):
    length = query.shape[1]
    score_scale = query.shape[3] ** (-0.5)
    delta = jnp.sum(grad_att.astype(jnp.float32) * attended.astype(jnp.float32), axis=-1)
    grad_keys = jnp.zeros(keys.shape, jnp.float32)
    grad_values = jnp.zeros(values.shape, jnp.float32)
    grad_query = []
    for offset in range(0, length, block_rows):
        q_block = query[:, offset : offset + block_rows]
        go_block = grad_att[:, offset : offset + block_rows]
        scores = (
            jnp.einsum("sqhd,skhd->shqk", q_block, keys, preferred_element_type=jnp.float32)
            * score_scale
        )
        allowed = block_mask(segment, offset, block_rows)
        scores = jnp.where(allowed[:, None], scores, -jnp.inf)
        lse_block = logsum[:, :, offset : offset + block_rows]
        pexact = jnp.exp(scores - lse_block[..., None])
        probs = pexact.astype(jnp.bfloat16)
        grad_values = grad_values + jnp.einsum(
            "shqk,sqhd->skhd", probs, go_block, preferred_element_type=jnp.float32
        )
        grad_probs = jnp.einsum(
            "sqhd,skhd->shqk", go_block, values, preferred_element_type=jnp.float32
        )
        delta_block = jnp.transpose(delta[:, offset : offset + block_rows], (0, 2, 1))[..., None]
        grad_scores = (pexact * (grad_probs - delta_block)).astype(jnp.bfloat16)
        grad_query.append(
            jnp.einsum("shqk,skhd->sqhd", grad_scores, keys, preferred_element_type=jnp.float32)
            * score_scale
        )
        grad_keys = (
            grad_keys
            + jnp.einsum(
                "shqk,sqhd->skhd", grad_scores, q_block, preferred_element_type=jnp.float32
            )
            * score_scale
        )
    return (jnp.concatenate(grad_query, axis=1), grad_keys, grad_values)


def split_three(values):
    high = lax.reduce_precision(values, exponent_bits=8, mantissa_bits=7)
    rest = values - high
    middle = lax.reduce_precision(rest, exponent_bits=8, mantissa_bits=7)
    low = rest - middle
    return jnp.stack([high, middle, low]).astype(jnp.bfloat16)


def join_three(parts):
    parts = parts.astype(jnp.float32)
    return (parts[0] + parts[1]) + parts[2]


def sum_over_dp(tree):
    dp_count = lax.axis_size("dp")
    step = 1
    while step < dp_count:
        pairs = [(i, i ^ step) for i in range(dp_count)]
        other = lax.ppermute(tree, "dp", pairs)
        tree = jax.tree.map(
            lambda mine, theirs: (mine.astype(jnp.float32) + theirs.astype(jnp.float32)).astype(
                mine.dtype
            ),
            tree,
            other,
        )
        step *= 2
    return tree


def local(
    layer_input,
    segment_ids,
    cotangent,
    norm1_gain,
    norm1_bias,
    norm2_gain,
    norm2_bias,
    w_qkv,
    b_qkv,
    w_out,
    w_up,
    b_up,
    w_down,
    out_bias,
):
    col_count = lax.axis_size("col")
    row_count = lax.axis_size("row")
    row_index = lax.axis_index("row")
    col_index = lax.axis_index("col")
    seq_count, rows_here, feat_here = layer_input.shape
    full_len = segment_ids.shape[1]
    model_width = feat_here * col_count
    head_dim = model_width // H
    rot_dims = head_dim // 4
    heads_here = b_qkv.shape[0] // (3 * head_dim)
    att_width = heads_here * head_dim
    qkv_here = b_qkv.shape[0]
    units_here = b_up.shape[0]
    in_width = qkv_here + units_here
    block_rows = min(512, full_len)
    pad_rows = 16

    w_in_parts = jnp.concatenate(
        [
            w_qkv.reshape(feat_here, col_count, qkv_here),
            w_up.reshape(feat_here, col_count, units_here),
        ],
        axis=2,
    )
    w_in_cols = lax.all_to_all(w_in_parts, "col", 1, 0, tiled=True).reshape(model_width, -1)
    w_qkv_cols = w_in_cols[:, :qkv_here]
    w_up_cols = w_in_cols[:, qkv_here:]
    w_back_parts = jnp.concatenate(
        [
            w_out.reshape(col_count, att_width, feat_here),
            w_down.reshape(col_count, units_here, feat_here),
        ],
        axis=1,
    )
    stacked_w = lax.all_to_all(w_back_parts, "col", 0, 2, tiled=True).reshape(-1, model_width)

    norm_code = split_three(jnp.stack([norm1_gain, norm1_bias, norm2_gain, norm2_bias]))
    norm_code = norm_code.reshape(12, feat_here)
    block = jnp.concatenate(
        [
            layer_input[0],
            cotangent[0],
            norm_code,
            jnp.zeros((pad_rows - 12, feat_here), jnp.bfloat16),
        ],
        axis=0,
    )
    gathered = lax.all_gather(block, ("row", "col"), axis=0, tiled=False)
    gathered = gathered.reshape(row_count, col_count, -1, feat_here)
    x_b = gathered[:, :, :rows_here].astype(jnp.float32)
    cot_b = gathered[:, :, rows_here : 2 * rows_here]
    norm_all = gathered[0, :, 2 * rows_here : 2 * rows_here + 12].transpose(1, 0, 2)
    norm_vals = join_three(norm_all.reshape(3, 4, col_count, 1, feat_here))
    gain1, bias1, gain2, bias2 = norm_vals[0], norm_vals[1], norm_vals[2], norm_vals[3]

    mean_val = jnp.mean(x_b, axis=(1, 3), keepdims=True)
    variance = jnp.mean(x_b * x_b, axis=(1, 3), keepdims=True) - mean_val * mean_val
    inv_std = lax.rsqrt(variance + NORM_EPS)
    normed = (x_b - mean_val) * inv_std
    first_in = (normed * gain1 + bias1).astype(jnp.bfloat16)
    second_in = (normed * gain2 + bias2).astype(jnp.bfloat16)
    w_qkv_b = w_qkv_cols.reshape(col_count, feat_here, qkv_here)
    w_up_b = w_up_cols.reshape(col_count, feat_here, units_here)
    stacked_b = stacked_w.reshape(-1, col_count, feat_here)
    qkv_sum = jnp.einsum("rcpf,cfk->rpk", first_in, w_qkv_b, preferred_element_type=jnp.float32)
    up_sum = jnp.einsum("rcpf,cfu->rpu", second_in, w_up_b, preferred_element_type=jnp.float32)
    cosine, sine = rope_tables(full_len, rot_dims)
    qkv = (qkv_sum + b_qkv).reshape(seq_count, full_len, heads_here, 3, head_dim)
    query = rotate(qkv[:, :, :, 0], cosine, sine, rot_dims).astype(jnp.bfloat16)
    keys = rotate(qkv[:, :, :, 1], cosine, sine, rot_dims).astype(jnp.bfloat16)
    values = qkv[:, :, :, 2].astype(jnp.bfloat16)
    attended, logsum = attend_forward(query, keys, values, segment_ids, block_rows)
    up_val = (up_sum + b_up).reshape(full_len, units_here)
    hidden = jax.nn.gelu(up_val, approximate=False).astype(jnp.bfloat16)
    joined = jnp.concatenate([attended.reshape(full_len, att_width), hidden], axis=1)
    joined = joined.reshape(row_count, rows_here, -1)
    branch_blocks = jnp.einsum(
        "rpm,mcf->rcpf", joined, stacked_b, preferred_element_type=jnp.float32
    ).astype(jnp.bfloat16)
    branch_sum = lax.psum_scatter(
        branch_blocks.reshape(row_count * col_count, rows_here, feat_here),
        ("row", "col"),
        scatter_dimension=0,
        tiled=True,
    )[0]
    layer_output = (
        layer_input[0].astype(jnp.float32) + branch_sum.astype(jnp.float32) + out_bias
    ).astype(jnp.bfloat16)[None]

    grad_stacked = jnp.einsum("rpm,rcpf->mcf", joined, cot_b, preferred_element_type=jnp.float32)
    joined_grad = jnp.einsum(
        "rcpf,mcf->rpm", cot_b, stacked_b, preferred_element_type=jnp.float32
    ).reshape(full_len, -1)
    grad_att = joined_grad[:, :att_width].astype(jnp.bfloat16).reshape(
        seq_count, full_len, heads_here, head_dim
    )
    grad_up = joined_grad[:, att_width:] * gelu_slope(up_val)
    grad_b_up = jnp.sum(grad_up, axis=0)
    up_round = grad_up.astype(jnp.bfloat16).reshape(row_count, rows_here, units_here)
    grad_w_up = jnp.einsum("rcpf,rpu->cfu", second_in, up_round, preferred_element_type=jnp.float32)

    up_grads = lax.all_to_all(
        grad_w_up.astype(jnp.bfloat16).reshape(model_width, 1, units_here), "col", 0, 1, tiled=True
    )
    back_grads = lax.all_to_all(
        grad_stacked.astype(jnp.bfloat16).reshape(1, -1, model_width), "col", 2, 0, tiled=True
    )
    up_grads, back_grads, grad_b_up = sum_over_dp((up_grads, back_grads, grad_b_up))

    grad_q, grad_k, grad_v = attend_backward(
        query, keys, values, attended, grad_att, logsum, segment_ids, block_rows
    )
    grad_q = inverse_rotation(grad_q, cosine, sine, rot_dims)
    grad_k = inverse_rotation(grad_k, cosine, sine, rot_dims)
    grad_qkv = jnp.stack([grad_q, grad_k, grad_v], axis=3).reshape(full_len, qkv_here)
    grad_b_qkv = jnp.sum(grad_qkv, axis=0)
    qkv_round = grad_qkv.astype(jnp.bfloat16).reshape(row_count, rows_here, qkv_here)
    grad_w_qkv = jnp.einsum(
        "rcpf,rpk->cfk", first_in, qkv_round, preferred_element_type=jnp.float32
    )
    part_first = jnp.einsum("rpk,cfk->rcpf", qkv_round, w_qkv_b, preferred_element_type=jnp.float32)
    part_second = jnp.einsum("rpu,cfu->rcpf", up_round, w_up_b, preferred_element_type=jnp.float32)
    part_normed = part_first * gain1 + part_second * gain2
    up_grads, back_grads, grad_b_up, part_normed = lax.optimization_barrier(
        (up_grads, back_grads, grad_b_up, part_normed)
    )

    gain_parts = jnp.stack(
        [
            jnp.sum(part_first * normed, axis=(0, 2)),
            jnp.sum(part_first, axis=(0, 2)),
            jnp.sum(part_second * normed, axis=(0, 2)),
            jnp.sum(part_second, axis=(0, 2)),
        ]
    )
    stat_rows = 2 * rows_here // feat_here
    stat_parts = jnp.stack(
        [jnp.sum(part_normed, axis=(1, 3)), jnp.sum(part_normed * normed, axis=(1, 3))], axis=1
    ).reshape(row_count, 1, stat_rows, feat_here)
    extra_rows = -(-(4 + stat_rows) // pad_rows) * pad_rows
    extras = jnp.concatenate(
        [
            jnp.broadcast_to(
                gain_parts.transpose(1, 0, 2)[None], (row_count, col_count, 4, feat_here)
            ),
            jnp.broadcast_to(stat_parts, (row_count, col_count, stat_rows, feat_here)),
            jnp.zeros(
                (row_count, col_count, extra_rows - 4 - stat_rows, feat_here), jnp.float32
            ),
        ],
        axis=2,
    ).astype(jnp.bfloat16)
    normed_blocks = jnp.concatenate([part_normed.astype(jnp.bfloat16), extras], axis=2)
    normed_blocks = normed_blocks.reshape(row_count * col_count, -1, feat_here)
    normed_sum = lax.psum_scatter(normed_blocks, ("row", "col"), scatter_dimension=0, tiled=True)[0]
    grad_normed = normed_sum[:rows_here].astype(jnp.float32)
    gain_sums = normed_sum[rows_here : rows_here + 4].astype(jnp.float32)
    stat_sums = normed_sum[rows_here + 4 : rows_here + 4 + stat_rows].astype(jnp.float32)
    stat_sums = stat_sums.reshape(2, rows_here)

    col_index = lax.axis_index("col")
    normed_here = lax.dynamic_slice(
        normed, (row_index, col_index, 0, 0), (1, 1, rows_here, feat_here)
    )[0, 0]
    inv_std_here = lax.dynamic_slice_in_dim(inv_std, row_index, 1, axis=0)[0, 0]
    grad_input = cotangent[0].astype(jnp.float32) + inv_std_here * (
        grad_normed
        - (stat_sums[0] / model_width)[:, None]
        - normed_here * (stat_sums[1] / model_width)[:, None]
    )

    cot_sum = lax.dynamic_slice_in_dim(
        jnp.sum(cot_b.astype(jnp.float32), axis=(0, 2)), col_index, 1, axis=0
    )[0]
    qkv_grads = lax.all_to_all(
        grad_w_qkv.astype(jnp.bfloat16).reshape(model_width, 1, qkv_here), "col", 0, 1, tiled=True
    )
    small = jnp.concatenate([grad_b_qkv, gain_sums.reshape(-1), cot_sum])
    qkv_grads, small = sum_over_dp((qkv_grads, small))
    up_grads = up_grads.astype(jnp.float32)
    qkv_grads = qkv_grads.astype(jnp.float32)
    back_grads = back_grads.astype(jnp.float32)
    grad_w_qkv_out = qkv_grads.reshape(feat_here, -1)
    grad_w_up_out = up_grads.reshape(feat_here, -1)
    grad_w_out_out = back_grads[:, :att_width].reshape(-1, feat_here)
    grad_w_down_out = back_grads[:, att_width:].reshape(-1, feat_here)
    vector_sums = small[qkv_here:].reshape(5, feat_here)
    return (
        layer_output,
        grad_input[None],
        grad_w_qkv_out,
        small[:qkv_here],
        grad_w_out_out,
        grad_w_up_out,
        grad_b_up,
        grad_w_down_out,
        vector_sums[4],
        vector_sums[0],
        vector_sums[1],
        vector_sums[2],
        vector_sums[3],
    )


def solution(mesh):
    in_specs = (
        P("dp", "row", "col"),
        P("dp", None),
        P("dp", "row", "col"),
        P("col"),
        P("col"),
        P("col"),
        P("col"),
        P("col", "row"),
        P(("row", "col")),
        P("row", "col"),
        P("col", "row"),
        P(("row", "col")),
        P("row", "col"),
        P("col"),
    )
    out_specs = (
        P("dp", "row", "col"),
        P("dp", "row", "col"),
        P("col", "row"),
        P(("row", "col")),
        P("row", "col"),
        P("col", "row"),
        P(("row", "col")),
        P("row", "col"),
        P("col"),
        P("col"),
        P("col"),
        P("col"),
        P("col"),
    )
    return jax.shard_map(local, mesh=mesh, in_specs=in_specs, out_specs=out_specs, check_vma=False)
```

```python
import math

import jax
import jax.numpy as jnp
from jax import lax
from jax.sharding import PartitionSpec as P

H = 16


NORM_EPS = 1e-05


def rope_tables(length, rot_dims):
    half_dims = rot_dims // 2
    position = jnp.arange(length).astype(jnp.float32)
    freqs = 10000.0 ** (-jnp.arange(half_dims).astype(jnp.float32) * 2.0 / rot_dims)
    angles = position[:, None] * freqs[None, :]
    return (jnp.cos(angles), jnp.sin(angles))


def rotate(values, cosine, sine, rot_dims):
    half_dims = rot_dims // 2
    lower_half = values[..., :half_dims]
    upper_half = values[..., half_dims:rot_dims]
    cos_b = cosine[None, :, None, :]
    sin_b = sine[None, :, None, :]
    return jnp.concatenate(
        [
            lower_half * cos_b - upper_half * sin_b,
            upper_half * cos_b + lower_half * sin_b,
            values[..., rot_dims:],
        ],
        axis=-1,
    )


def inverse_rotation(grads, cosine, sine, rot_dims):
    half_dims = rot_dims // 2
    lower_half = grads[..., :half_dims]
    upper_half = grads[..., half_dims:rot_dims]
    cos_b = cosine[None, :, None, :]
    sin_b = sine[None, :, None, :]
    return jnp.concatenate(
        [
            lower_half * cos_b + upper_half * sin_b,
            upper_half * cos_b - lower_half * sin_b,
            grads[..., rot_dims:],
        ],
        axis=-1,
    )


def gelu_slope(values):
    cdf_part = 0.5 * (1.0 + lax.erf(values * (1.0 / math.sqrt(2.0))))
    return cdf_part + values * jnp.exp(-0.5 * values * values) * (1.0 / math.sqrt(2.0 * math.pi))


def block_mask(segment, offset, block_rows):
    length = segment.shape[1]
    position = jnp.arange(length)
    causal = position[offset : offset + block_rows, None] >= position[None, :]
    same_doc = segment[:, offset : offset + block_rows, None] == segment[:, None, :]
    return causal[None] & same_doc


def attend_forward(query, keys, values, segment, block_rows):
    length = query.shape[1]
    score_scale = query.shape[3] ** (-0.5)
    outputs = []
    totals = []
    for offset in range(0, length, block_rows):
        q_block = query[:, offset : offset + block_rows]
        scores = (
            jnp.einsum("sqhd,skhd->shqk", q_block, keys, preferred_element_type=jnp.float32)
            * score_scale
        )
        allowed = block_mask(segment, offset, block_rows)
        scores = jnp.where(allowed[:, None], scores, -jnp.inf)
        row_peak = jnp.max(scores, axis=-1, keepdims=True)
        logsum = row_peak + jnp.log(jnp.sum(jnp.exp(scores - row_peak), axis=-1, keepdims=True))
        weights = jnp.exp(scores - logsum).astype(jnp.bfloat16)
        block_out = jnp.einsum(
            "shqk,skhd->sqhd", weights, values, preferred_element_type=jnp.float32
        )
        outputs.append(block_out.astype(jnp.bfloat16))
        totals.append(logsum[..., 0])
    return (jnp.concatenate(outputs, axis=1), jnp.concatenate(totals, axis=2))


def attend_backward(query, keys, values, attended, grad_att, logsum, segment, block_rows):
    length = query.shape[1]
    score_scale = query.shape[3] ** (-0.5)
    delta = jnp.sum(grad_att.astype(jnp.float32) * attended.astype(jnp.float32), axis=-1)
    grad_keys = jnp.zeros(keys.shape, jnp.float32)
    grad_values = jnp.zeros(values.shape, jnp.float32)
    grad_query = []
    for offset in range(0, length, block_rows):
        q_block = query[:, offset : offset + block_rows]
        go_block = grad_att[:, offset : offset + block_rows]
        scores = (
            jnp.einsum("sqhd,skhd->shqk", q_block, keys, preferred_element_type=jnp.float32)
            * score_scale
        )
        allowed = block_mask(segment, offset, block_rows)
        scores = jnp.where(allowed[:, None], scores, -jnp.inf)
        lse_block = logsum[:, :, offset : offset + block_rows]
        pexact = jnp.exp(scores - lse_block[..., None])
        probs = pexact.astype(jnp.bfloat16)
        grad_values = grad_values + jnp.einsum(
            "shqk,sqhd->skhd", probs, go_block, preferred_element_type=jnp.float32
        )
        grad_probs = jnp.einsum(
            "sqhd,skhd->shqk", go_block, values, preferred_element_type=jnp.float32
        )
        delta_block = jnp.transpose(delta[:, offset : offset + block_rows], (0, 2, 1))[..., None]
        grad_scores = (pexact * (grad_probs - delta_block)).astype(jnp.bfloat16)
        grad_query.append(
            jnp.einsum("shqk,skhd->sqhd", grad_scores, keys, preferred_element_type=jnp.float32)
            * score_scale
        )
        grad_keys = (
            grad_keys
            + jnp.einsum(
                "shqk,sqhd->skhd", grad_scores, q_block, preferred_element_type=jnp.float32
            )
            * score_scale
        )
    return (jnp.concatenate(grad_query, axis=1), grad_keys, grad_values)


def split_three(values):
    high = lax.reduce_precision(values, exponent_bits=8, mantissa_bits=7)
    rest = values - high
    middle = lax.reduce_precision(rest, exponent_bits=8, mantissa_bits=7)
    low = rest - middle
    return jnp.stack([high, middle, low]).astype(jnp.bfloat16)


def join_three(parts):
    parts = parts.astype(jnp.float32)
    return (parts[0] + parts[1]) + parts[2]


def sum_over_dp(tree):
    dp_count = lax.axis_size("dp")
    dp_index = lax.axis_index("dp")
    leaves, treedef = jax.tree.flatten(tree)
    steps = []
    step = 1
    while step < dp_count:
        steps.append(step)
        step *= 2
    for step in steps:
        bit = (dp_index // step) % 2
        pairs = [(i, i ^ step) for i in range(dp_count)]
        keeps, sends = [], []
        for leaf in leaves:
            half = leaf.shape[0] // 2
            keeps.append(lax.dynamic_slice_in_dim(leaf, bit * half, half, axis=0))
            sends.append(lax.dynamic_slice_in_dim(leaf, (1 - bit) * half, half, axis=0))
        received = lax.ppermute(sends, "dp", pairs)
        leaves = [
            (mine.astype(jnp.float32) + theirs.astype(jnp.float32)).astype(mine.dtype)
            for mine, theirs in zip(keeps, received)
        ]
    for step in reversed(steps):
        bit = (dp_index // step) % 2
        pairs = [(i, i ^ step) for i in range(dp_count)]
        received = lax.ppermute(leaves, "dp", pairs)
        joined = []
        for mine, theirs in zip(leaves, received):
            size = mine.shape[0]
            both = jnp.zeros((2 * size,) + mine.shape[1:], mine.dtype)
            both = lax.dynamic_update_slice_in_dim(both, mine, bit * size, axis=0)
            both = lax.dynamic_update_slice_in_dim(both, theirs, (1 - bit) * size, axis=0)
            joined.append(both)
        leaves = joined
    return jax.tree.unflatten(treedef, leaves)


def local(
    layer_input,
    segment_ids,
    cotangent,
    norm1_gain,
    norm1_bias,
    norm2_gain,
    norm2_bias,
    w_qkv,
    b_qkv,
    w_out,
    w_up,
    b_up,
    w_down,
    out_bias,
):
    col_count = lax.axis_size("col")
    row_count = lax.axis_size("row")
    row_index = lax.axis_index("row")
    col_index = lax.axis_index("col")
    seq_count, rows_here, feat_here = layer_input.shape
    full_len = segment_ids.shape[1]
    model_width = feat_here * col_count
    head_dim = model_width // H
    rot_dims = head_dim // 4
    heads_here = b_qkv.shape[0] // (3 * head_dim)
    att_width = heads_here * head_dim
    qkv_here = b_qkv.shape[0]
    units_here = b_up.shape[0]
    in_width = qkv_here + units_here
    block_rows = min(512, full_len)
    pad_rows = 16

    w_in_parts = jnp.concatenate(
        [
            w_qkv.reshape(feat_here, col_count, qkv_here),
            w_up.reshape(feat_here, col_count, units_here),
        ],
        axis=2,
    )
    w_in_cols = lax.all_to_all(w_in_parts, "col", 1, 0, tiled=True).reshape(model_width, -1)
    w_qkv_cols = w_in_cols[:, :qkv_here]
    w_up_cols = w_in_cols[:, qkv_here:]
    w_back_parts = jnp.concatenate(
        [
            w_out.reshape(col_count, att_width, feat_here),
            w_down.reshape(col_count, units_here, feat_here),
        ],
        axis=1,
    )
    stacked_w = lax.all_to_all(w_back_parts, "col", 0, 2, tiled=True).reshape(-1, model_width)

    norm_code = split_three(jnp.stack([norm1_gain, norm1_bias, norm2_gain, norm2_bias]))
    norm_code = norm_code.reshape(12, feat_here)
    block = jnp.concatenate(
        [
            layer_input[0],
            cotangent[0],
            norm_code,
            jnp.zeros((pad_rows - 12, feat_here), jnp.bfloat16),
        ],
        axis=0,
    )
    gathered = lax.all_gather(block, ("row", "col"), axis=0, tiled=False)
    gathered = gathered.reshape(row_count, col_count, -1, feat_here)

    def full_array(first_row):
        part = gathered[:, :, first_row : first_row + rows_here]
        return part.transpose(0, 2, 1, 3).reshape(row_count * rows_here, model_width)

    x_full = full_array(0).astype(jnp.float32)
    cot_full = full_array(rows_here)
    norm_all = gathered[0, :, 2 * rows_here : 2 * rows_here + 12].transpose(1, 0, 2)
    norm_vals = join_three(norm_all.reshape(3, 4, model_width))
    gain1, bias1, gain2, bias2 = norm_vals[0], norm_vals[1], norm_vals[2], norm_vals[3]

    mean_val = jnp.mean(x_full, axis=1, keepdims=True)
    variance = jnp.mean(x_full * x_full, axis=1, keepdims=True) - mean_val * mean_val
    inv_std = lax.rsqrt(variance + NORM_EPS)
    normed = (x_full - mean_val) * inv_std
    first_in = (normed * gain1 + bias1).astype(jnp.bfloat16)
    second_in = (normed * gain2 + bias2).astype(jnp.bfloat16)
    qkv_sum = jnp.dot(first_in, w_qkv_cols, preferred_element_type=jnp.float32)
    up_sum = jnp.dot(second_in, w_up_cols, preferred_element_type=jnp.float32)
    cosine, sine = rope_tables(full_len, rot_dims)
    qkv = (qkv_sum + b_qkv).reshape(seq_count, full_len, heads_here, 3, head_dim)
    query = rotate(qkv[:, :, :, 0], cosine, sine, rot_dims).astype(jnp.bfloat16)
    keys = rotate(qkv[:, :, :, 1], cosine, sine, rot_dims).astype(jnp.bfloat16)
    values = qkv[:, :, :, 2].astype(jnp.bfloat16)
    attended, logsum = attend_forward(query, keys, values, segment_ids, block_rows)
    up_val = up_sum + b_up
    hidden = jax.nn.gelu(up_val, approximate=False).astype(jnp.bfloat16)
    joined = jnp.concatenate([attended.reshape(full_len, att_width), hidden], axis=1)
    branch_part = jnp.dot(joined, stacked_w, preferred_element_type=jnp.float32)
    branch_blocks = (
        branch_part.astype(jnp.bfloat16)
        .reshape(row_count, rows_here, col_count, feat_here)
        .transpose(0, 2, 1, 3)
        .reshape(row_count * col_count, rows_here, feat_here)
    )
    branch_sum = lax.psum_scatter(branch_blocks, ("row", "col"), scatter_dimension=0, tiled=True)[0]
    layer_output = (
        layer_input[0].astype(jnp.float32) + branch_sum.astype(jnp.float32) + out_bias
    ).astype(jnp.bfloat16)[None]

    grad_stacked = jnp.dot(joined.T, cot_full, preferred_element_type=jnp.float32)
    joined_grad = jnp.dot(cot_full, stacked_w.T, preferred_element_type=jnp.float32)
    grad_att = joined_grad[:, :att_width].astype(jnp.bfloat16).reshape(
        seq_count, full_len, heads_here, head_dim
    )
    grad_up = joined_grad[:, att_width:] * gelu_slope(up_val)
    grad_q, grad_k, grad_v = attend_backward(
        query, keys, values, attended, grad_att, logsum, segment_ids, block_rows
    )
    grad_q = inverse_rotation(grad_q, cosine, sine, rot_dims)
    grad_k = inverse_rotation(grad_k, cosine, sine, rot_dims)
    grad_qkv = jnp.stack([grad_q, grad_k, grad_v], axis=3).reshape(full_len, qkv_here)
    grad_b_qkv = jnp.sum(grad_qkv, axis=0)
    grad_b_up = jnp.sum(grad_up, axis=0)
    qkv_round = grad_qkv.astype(jnp.bfloat16)
    up_round = grad_up.astype(jnp.bfloat16)
    grad_w_qkv = jnp.dot(first_in.T, qkv_round, preferred_element_type=jnp.float32)
    grad_w_up = jnp.dot(second_in.T, up_round, preferred_element_type=jnp.float32)
    part_first = jnp.einsum(
        "rpk,cfk->rcpf",
        qkv_round.reshape(row_count, rows_here, qkv_here),
        w_qkv_cols.reshape(col_count, feat_here, qkv_here),
        preferred_element_type=jnp.float32,
    )
    part_second = jnp.einsum(
        "rpu,cfu->rcpf",
        up_round.reshape(row_count, rows_here, units_here),
        w_up_cols.reshape(col_count, feat_here, units_here),
        preferred_element_type=jnp.float32,
    )
    block_shape = (row_count, rows_here, col_count, feat_here)
    normed_b = normed.reshape(block_shape).transpose(0, 2, 1, 3)
    gain1_b = gain1.reshape(1, col_count, 1, feat_here)
    gain2_b = gain2.reshape(1, col_count, 1, feat_here)
    part_normed = part_first * gain1_b + part_second * gain2_b

    gain_parts = jnp.stack(
        [
            jnp.sum(part_first * normed_b, axis=(0, 2)),
            jnp.sum(part_first, axis=(0, 2)),
            jnp.sum(part_second * normed_b, axis=(0, 2)),
            jnp.sum(part_second, axis=(0, 2)),
        ]
    )
    stat_parts = jnp.stack(
        [jnp.sum(part_normed, axis=(1, 3)), jnp.sum(part_normed * normed_b, axis=(1, 3))]
    ).reshape(2, row_count, rows_here // feat_here, feat_here)
    stat_rows = 2 * rows_here // feat_here
    stat_parts = stat_parts.transpose(1, 0, 2, 3).reshape(row_count, 1, stat_rows, feat_here)
    extra_rows = -(-(4 + stat_rows) // pad_rows) * pad_rows
    extras = jnp.concatenate(
        [
            jnp.broadcast_to(
                gain_parts.transpose(1, 0, 2)[None], (row_count, col_count, 4, feat_here)
            ),
            jnp.broadcast_to(stat_parts, (row_count, col_count, stat_rows, feat_here)),
            jnp.zeros(
                (row_count, col_count, extra_rows - 4 - stat_rows, feat_here), jnp.float32
            ),
        ],
        axis=2,
    ).astype(jnp.bfloat16)
    normed_blocks = jnp.concatenate([part_normed.astype(jnp.bfloat16), extras], axis=2)
    normed_blocks = normed_blocks.reshape(row_count * col_count, -1, feat_here)
    normed_sum = lax.psum_scatter(normed_blocks, ("row", "col"), scatter_dimension=0, tiled=True)[0]
    grad_normed = normed_sum[:rows_here].astype(jnp.float32)
    gain_sums = normed_sum[rows_here : rows_here + 4].astype(jnp.float32)
    stat_sums = normed_sum[rows_here + 4 : rows_here + 4 + stat_rows].astype(jnp.float32)
    stat_sums = stat_sums.reshape(2, rows_here)

    row_start = row_index * rows_here
    normed_here = lax.dynamic_slice(
        normed, (row_start, col_index * feat_here), (rows_here, feat_here)
    )
    inv_std_here = lax.dynamic_slice(inv_std, (row_start, 0), (rows_here, 1))
    grad_input = cotangent[0].astype(jnp.float32) + inv_std_here * (
        grad_normed
        - (stat_sums[0] / model_width)[:, None]
        - normed_here * (stat_sums[1] / model_width)[:, None]
    )

    cot_sum = lax.dynamic_slice_in_dim(
        jnp.sum(cot_full.astype(jnp.float32), axis=0), col_index * feat_here, feat_here
    )
    in_grads = jnp.concatenate([grad_w_qkv, grad_w_up], axis=1).astype(jnp.bfloat16)
    in_grads = lax.all_to_all(
        in_grads.reshape(model_width, 1, in_width), "col", 0, 1, tiled=True
    )
    back_grads = lax.all_to_all(
        grad_stacked.astype(jnp.bfloat16).reshape(1, -1, model_width), "col", 2, 0, tiled=True
    )
    small = jnp.concatenate([grad_b_qkv, grad_b_up, gain_sums.reshape(-1), cot_sum])
    small_len = small.shape[0]
    dp_count = lax.axis_size("dp")
    small_pad = -(-small_len // (8 * dp_count)) * 8 * dp_count
    small = jnp.pad(small, (0, small_pad - small_len)).reshape(dp_count * 8, -1)
    in_grads, back_grads, small = sum_over_dp((in_grads, back_grads, small))
    small = small.reshape(-1)[:small_len]
    in_grads = in_grads.astype(jnp.float32)
    back_grads = back_grads.astype(jnp.float32)
    grad_w_qkv_out = in_grads[:, :, :qkv_here].reshape(feat_here, -1)
    grad_w_up_out = in_grads[:, :, qkv_here:].reshape(feat_here, -1)
    grad_w_out_out = back_grads[:, :att_width].reshape(-1, feat_here)
    grad_w_down_out = back_grads[:, att_width:].reshape(-1, feat_here)
    vector_sums = small[in_width:].reshape(5, feat_here)
    return (
        layer_output,
        grad_input[None],
        grad_w_qkv_out,
        small[:qkv_here],
        grad_w_out_out,
        grad_w_up_out,
        small[qkv_here:in_width],
        grad_w_down_out,
        vector_sums[4],
        vector_sums[0],
        vector_sums[1],
        vector_sums[2],
        vector_sums[3],
    )


def solution(mesh):
    in_specs = (
        P("dp", "row", "col"),
        P("dp", None),
        P("dp", "row", "col"),
        P("col"),
        P("col"),
        P("col"),
        P("col"),
        P("col", "row"),
        P(("row", "col")),
        P("row", "col"),
        P("col", "row"),
        P(("row", "col")),
        P("row", "col"),
        P("col"),
    )
    out_specs = (
        P("dp", "row", "col"),
        P("dp", "row", "col"),
        P("col", "row"),
        P(("row", "col")),
        P("row", "col"),
        P("col", "row"),
        P(("row", "col")),
        P("row", "col"),
        P("col"),
        P("col"),
        P("col"),
        P("col"),
        P("col"),
    )
    return jax.shard_map(local, mesh=mesh, in_specs=in_specs, out_specs=out_specs, check_vma=False)
```
